512 devices in a mesh: seq: 128 (over z, y, core), head: 4 (over x).
Axes of the slice: x: 4, y: 4, z: 16, core: 2. Of those that a mesh axis runs over, the one named last changes fastest.
Arguments:
- queries: bfloat16 [49152, 1536], P('seq', 'head'), may hold values from -34.5 to 34.5
- out_grad: bfloat16 [49152, 1536], P('seq', 'head'), may hold values from -48 to 48
- tile_mask: int32 [384, 2], P('seq'), may hold values from 0 to 1, as said below
- slot_caption: int32 [128, 2], replicated, may hold values from 0 to 32, as said below
- caption_cache: bfloat16 [2, 256, 512, 1536], P(None, 'seq', None, 'head'), may hold values from -6.1 to 6.1, as said below
- key_weight: bfloat16 [1536, 1536], P(None, 'head'), may hold values from -0.15625 to 0.15625
- value_weight: bfloat16 [1536, 1536], P(None, 'head'), may hold values from -0.15625 to 0.15625
Outputs:
- query_grad: bfloat16 [49152, 1536], P('seq', 'head')
- text_grad: bfloat16 [32, 512, 1536], P(None, 'seq', 'head')
The draws below stay inside these ranges and needn't reach their ends.
Inputs may be any that keep to these rules, and one draw needn't show every extreme that they name: `tile_mask`: each row has exactly one 1; it marks the slot of its seq index whose caption the tile reads. `slot_caption`: row d lists the captions that the tiles of seq index d read, each once; one entry always names a caption, the other names another caption or is 32 for an empty slot, and no tile points to an empty slot. A caption's tiles are consecutive and lie on consecutive seq indices; a seq index holds at most one caption boundary; every caption is read. `caption_cache`: slots that hold the same caption hold equal copies of its keys and values.
All inputs are finite; a program needn't handle non-finite values.
Results may differ from the reference program's by a relative error of at most 0.0096.
Values may be sent and summed in bfloat16 or wider, within the bound.
A program may use at most 64 MiB of HBM per device.

```python
import jax
import jax.numpy as jnp
from jax import lax

D = 1536
HEADS = 12
DH = 128
L = 512
TILE = 128
SLOTS = 2
SPAN = 4
TOKENS = 49152
TILES_DEV = 3
CAPS = 32
HD = 1536
N_SEQ = 128


def caption_layout(key):
    base_key = jax.random.fold_in(key, 101)
    offsets = jax.random.randint(jax.random.fold_in(base_key, 1), (N_SEQ,), 0, TILES_DEV)
    forced = jax.random.randint(jax.random.fold_in(base_key, 2), (), 1, TILES_DEV)
    swapped = jax.random.randint(jax.random.fold_in(base_key, 4), (N_SEQ,), 0, 2).astype(jnp.int32)
    device = jnp.arange(N_SEQ, dtype=jnp.int32)
    starts = (device % SPAN == 0) & (device > 0)
    offsets = jnp.where(device == SPAN, forced, offsets)
    offsets = jnp.where(starts, offsets, 0).astype(jnp.int32)
    labels = jax.random.permutation(jax.random.fold_in(base_key, 3), CAPS).astype(jnp.int32)
    tile_index = jnp.arange(N_SEQ * TILES_DEV, dtype=jnp.int32)
    tile_device = tile_index // TILES_DEV
    local_index = tile_index % TILES_DEV
    later_part = (local_index >= offsets[tile_device]).astype(jnp.int32)
    own_slot = jnp.where(swapped[tile_device] == 1, 1 - later_part, later_part).astype(jnp.int32)
    device_group = device // SPAN
    earlier = jnp.where(offsets > 0, labels[jnp.maximum(device_group - 1, 0)], CAPS)
    current = labels[device_group]
    first_col = jnp.where(swapped == 1, current, earlier)
    second_col = jnp.where(swapped == 1, earlier, current)
    slot_table = jnp.stack([first_col, second_col], axis=1).astype(jnp.int32)
    return (own_slot, slot_table)


def caption_values(key):
    base_key = jax.random.fold_in(key, 202)
    drawn = jnp.clip(jax.random.normal(base_key, (2, CAPS, L, HD), jnp.float32), -6.0, 6.0)
    return drawn


def draw_tile_mask(key, part):
    own_slot, slot_table = caption_layout(key)
    return (own_slot[:, None] == jnp.arange(SLOTS, dtype=jnp.int32)[None, :]).astype(jnp.int32)


def draw_slot_caption(key, part):
    own_slot, slot_table = caption_layout(key)
    return slot_table


def draw_caption_cache(key, part):
    drawn = caption_values(key)
    own_slot, slot_table = caption_layout(key)
    picked = jnp.minimum(slot_table, CAPS - 1).reshape(-1)
    return drawn[:, picked].astype(jnp.bfloat16)


def draw_queries(key, part):
    base_key = jax.random.fold_in(key, 404)
    result = jnp.clip(jax.random.normal(base_key, (TOKENS, HD), jnp.float32), -6.0, 6.0)
    return result.astype(jnp.bfloat16)


def block_scale(rng, dims, cuts, least, top_value):
    def one(dim, shards_of):
        heights = jax.random.uniform(jax.random.fold_in(jax.random.fold_in(rng, 6), dim), (shards_of,), jnp.float32, least / len(cuts), top_value / len(cuts))
        return jnp.repeat(jnp.exp(heights), dims[dim] // shards_of).reshape((-1,) + (1,) * (len(dims) - dim - 1))

    loudness = one(*cuts[0])
    for cut in cuts[1:]:
        loudness = loudness * one(*cut)
    return loudness


def gaussian(stream_key, shape, scale, reach, split=(), kind=jnp.bfloat16):
    values = scale * jax.random.normal(stream_key, shape, jnp.float32)
    if split:
        values = values * block_scale(stream_key, shape, split, -0.22, 0.18)
    return jnp.clip(values, -reach, reach).astype(kind)


def setup_inputs(seed: int = 0) -> dict:
    arg_keys = jax.random.split(jax.random.key(seed), 8)
    queries = draw_queries(jax.random.fold_in(arg_keys[7], 71), 0)
    out_grad = gaussian(arg_keys[1], (TOKENS, HD), 8.0, 48.0, ((0, 128), (1, 4)))
    tile_mask = draw_tile_mask(jax.random.fold_in(arg_keys[7], 71), 0)
    slot_caption = draw_slot_caption(jax.random.fold_in(arg_keys[7], 71), 0)
    caption_cache = draw_caption_cache(jax.random.fold_in(arg_keys[7], 71), 0)
    key_weight = gaussian(arg_keys[5], (D, HD), D ** -0.5, 0.15625, ((1, 4),))
    value_weight = gaussian(arg_keys[6], (D, HD), D ** -0.5, 0.15625, ((1, 4),))
    return dict(queries=queries, out_grad=out_grad, tile_mask=tile_mask, slot_caption=slot_caption, caption_cache=caption_cache, key_weight=key_weight, value_weight=value_weight)


def tile_gradients(query_tiles, grad_tiles, slot_mask, cache_rows):
    highest = lax.Precision.HIGHEST
    inv_root = 1.0 / (DH ** 0.5)
    slot_index = jnp.sum(slot_mask * jnp.arange(SLOTS, dtype=jnp.int32)[None, :], axis=1)
    key_rows = cache_rows[0][slot_index].astype(jnp.float32)
    value_rows = cache_rows[1][slot_index].astype(jnp.float32)
    query_f = query_tiles.astype(jnp.float32)
    grad_f = grad_tiles.astype(jnp.float32)
    scores = jnp.einsum("tqhe,tjhe->thqj", query_f, key_rows, precision=highest) * inv_root
    row_max = jnp.max(scores, axis=-1, keepdims=True)
    exp_scores = jnp.exp(scores - row_max)
    attention = exp_scores / jnp.sum(exp_scores, axis=-1, keepdims=True)
    attention_lo = attention.astype(jnp.bfloat16).astype(jnp.float32)
    context = jnp.einsum("thqj,tjhe->tqhe", attention_lo, value_rows, precision=highest)
    row_dot = jnp.transpose(jnp.sum(grad_f * context, axis=-1), (0, 2, 1))
    attention_grad = jnp.einsum("tqhe,tjhe->thqj", grad_f, value_rows, precision=highest)
    score_grad = attention * (attention_grad - row_dot[..., None])
    score_lo = score_grad.astype(jnp.bfloat16).astype(jnp.float32)
    query_grad = (jnp.einsum("thqj,tjhe->tqhe", score_lo, key_rows, precision=highest) * inv_root).astype(jnp.bfloat16)
    key_pieces = jnp.einsum("thqj,tqhe->tjhe", score_lo, query_f, precision=highest) * inv_root
    value_pieces = jnp.einsum("thqj,tqhe->tjhe", attention_lo, grad_f, precision=highest)
    slot_onehot = slot_mask.astype(jnp.float32)
    key_part = jnp.einsum("ts,tjhe->sjhe", slot_onehot, key_pieces, precision=highest).astype(jnp.bfloat16)
    value_part = jnp.einsum("ts,tjhe->sjhe", slot_onehot, value_pieces, precision=highest).astype(jnp.bfloat16)
    return query_grad, key_part, value_part


def reference(queries, out_grad, tile_mask, slot_caption, caption_cache, key_weight, value_weight):
    highest = lax.Precision.HIGHEST
    query_all = queries.reshape(N_SEQ, TILES_DEV, TILE, HEADS, DH)
    grad_all = out_grad.reshape(N_SEQ, TILES_DEV, TILE, HEADS, DH)
    mask_all = tile_mask.reshape(N_SEQ, TILES_DEV, SLOTS)

    def device_step(totals, device):
        cache_rows = lax.dynamic_slice_in_dim(caption_cache, device * SLOTS, SLOTS, axis=1)
        cache_rows = cache_rows.reshape(2, SLOTS, L, HEADS, DH)
        query_grad, key_part, value_part = tile_gradients(query_all[device], grad_all[device], mask_all[device], cache_rows)
        captions_of = slot_caption[device]
        live_mask = (captions_of < CAPS).astype(jnp.float32)[:, None, None, None]
        clamped = jnp.minimum(captions_of, CAPS - 1).astype(jnp.int32)
        totals = totals.at[0, clamped].add(key_part.astype(jnp.float32) * live_mask)
        totals = totals.at[1, clamped].add(value_part.astype(jnp.float32) * live_mask)
        return totals, query_grad

    start = jnp.zeros((2, CAPS, L, HEADS, DH), jnp.float32)
    totals, query_grads = lax.scan(device_step, start, jnp.arange(N_SEQ, dtype=jnp.int32))
    key_total = totals[0].reshape(CAPS * L, HD)
    value_total = totals[1].reshape(CAPS * L, HD)
    text_grad = jnp.dot(key_total, key_weight.astype(jnp.float32).T, precision=highest)
    text_grad = text_grad + jnp.dot(value_total, value_weight.astype(jnp.float32).T, precision=highest)
    text_grad = text_grad.reshape(CAPS, L, D).astype(jnp.bfloat16)
    return query_grads.reshape(TOKENS, HD), text_grad
```

```python
import functools
import math

import jax
import jax.numpy as jnp
from jax import lax
from jax.experimental import pallas as pl
from jax.experimental.pallas import tpu as pltpu
from jax.sharding import PartitionSpec as P

DH = 128
L = 512
TILE = 128
NT = 3
NH = 3
NX = 4
NY = 4
NZ = 16
NC = 2
ROWS = 4
GROUP = 4
CAPS = 32
HD = NH * DH
INV_ROOT = 1.0 / math.sqrt(DH)
MESH = pl.DeviceIdType.MESH
F32 = jnp.float32
BF16 = jnp.bfloat16
NT_DIMS = (((1,), (1,)), ((), ()))
TN_DIMS = (((0,), (0,)), ((), ()))
ORDER = [NZ // 2 + j // 2 if j % 2 == 0 else NZ // 2 - (j + 1) // 2 for j in range(NZ)]


def one_hot(rows, columns):
    return jnp.where(rows == columns, 1.0, 0.0).astype(BF16)


def kernel(
    meta, capcol, q_hbm, g_hbm, cache_hbm, kw_hbm, vw_hbm,
    qg_hbm, text_ref, parts_hbm,
    q_v, g_v, raw, kvp, w_v, qg_v, ds_s, at_s, parts, prx, pm, yrx, x_s, tsend, xrx, town, zsend, zrx,
    load_sem, store_sem, ps, pr, ys, yr, xs, xr, zs, zr,
):
    seq = lax.axis_index("seq")
    x = lax.axis_index("head")
    core = lax.rem(seq, 2)
    y = lax.rem(seq // 2, NY)
    z = seq // (2 * NY)

    def seq_of(z_, y_, core_):
        return (z_ * NY + y_) * 2 + core_

    pair_id = (seq_of(z, y, 1 - core), x)
    y_ids = [(seq_of(z, lax.rem(y + k, NY), core), x) for k in range(1, NY)]
    x_ids = [(seq, lax.rem(x + k, NX)) for k in range(1, NX)]
    z_ids = [(seq_of(lax.rem(z + k, NZ), y, core), x) for k in ORDER[:-1]]

    loads = []
    for kv in range(2):
        for s in range(2):
            loads.append(
                pltpu.make_async_copy(cache_hbm.at[kv, s], raw.at[kv, s], load_sem.at[kv * 2 + s])
            )
    loads.append(pltpu.make_async_copy(q_hbm, q_v, load_sem.at[4]))
    loads.append(pltpu.make_async_copy(g_hbm, g_v, load_sem.at[5]))
    loads.append(pltpu.make_async_copy(kw_hbm, w_v.at[0], load_sem.at[6]))
    loads.append(pltpu.make_async_copy(vw_hbm, w_v.at[1], load_sem.at[7]))
    for load in loads:
        load.start()

    barrier = pltpu.get_barrier_semaphore()
    partners = [pair_id] + y_ids + x_ids + z_ids
    for partner in partners:
        pl.semaphore_signal(barrier, inc=1, device_id=partner, device_id_type=MESH)

    n = lax.broadcasted_iota(jnp.int32, (L, L), 0)
    place = (n >> 2) & (NZ - 1)
    half = place >> 1
    dist = jnp.where((place & 1) == 0, NZ // 2 + half, NZ // 2 - 1 - half)
    zdest = (z + dist) & (NZ - 1)
    old = zdest * 32 + ((n >> 6) & 3) * 8 + (n >> 8) * 4 + (n & 3)
    perm = one_hot(old, lax.broadcasted_iota(jnp.int32, (L, L), 1))
    for kv in range(2):
        for s in range(2):
            loads[kv * 2 + s].wait()
            moved = jnp.dot(perm, raw[kv, s], preferred_element_type=F32).astype(BF16)
            for h in range(NH):
                kvp[s, h, :, kv * DH : (kv + 1) * DH] = moved[:, h * DH : (h + 1) * DH]
    loads[4].wait()
    loads[5].wait()

    def pair_copy(h):
        return pltpu.make_async_remote_copy(
            src_ref=parts.at[h, 1 - core], dst_ref=prx.at[h],
            send_sem=ps.at[h], recv_sem=pr.at[h],
            device_id=pair_id, device_id_type=MESH,
        )

    def y_copy(h, k, source):
        return pltpu.make_async_remote_copy(
            src_ref=pm.at[h, lax.rem(y + k, NY)], dst_ref=yrx.at[h, source],
            send_sem=ys.at[h, k - 1], recv_sem=yr.at[h, k - 1],
            device_id=y_ids[k - 1], device_id_type=MESH,
        )

    def x_copy(k, c):
        return pltpu.make_async_remote_copy(
            src_ref=tsend.at[k - 1, c], dst_ref=xrx.at[k - 1, c],
            send_sem=xs.at[k - 1, c], recv_sem=xr.at[k - 1, c],
            device_id=x_ids[k - 1], device_id_type=MESH,
        )

    def z_copy(j, source):
        return pltpu.make_async_remote_copy(
            src_ref=zsend.at[j], dst_ref=zrx.at[source],
            send_sem=zs.at[j], recv_sem=zr.at[j],
            device_id=z_ids[j], device_id_type=MESH,
        )

    def attend(h, t):
        rows = slice(t * TILE, (t + 1) * TILE)
        cols = slice(h * DH, (h + 1) * DH)
        kv = kvp[meta[t], h]
        q = q_v[rows, cols]
        g = g_v[rows, cols]
        zero = jnp.zeros_like(q)
        both = jnp.concatenate(
            [jnp.concatenate([q, zero], axis=1), jnp.concatenate([zero, g], axis=1)], axis=0
        )
        res = lax.dot_general(kv, both, NT_DIMS, preferred_element_type=F32)
        scores = res[:, :TILE] * INV_ROOT
        grads = res[:, TILE:]
        e = jnp.exp(scores - jnp.max(scores, axis=0, keepdims=True))
        att = e * (1.0 / jnp.sum(e, axis=0, keepdims=True))
        att_lo = att.astype(BF16)
        row_dot = jnp.sum(att_lo.astype(F32) * grads, axis=0, keepdims=True)
        ds = (att * (grads - row_dot)).astype(BF16)
        at_s[h, :, rows] = att_lo
        ds_s[h, :, rows] = ds
        qg = lax.dot_general(ds, kv[:, :DH], TN_DIMS, preferred_element_type=F32) * INV_ROOT
        qg_v[rows, cols] = qg.astype(BF16)

    def masked(ref, h):
        tiles = []
        for t in range(NT):
            v = ref[t * TILE : (t + 1) * TILE, h * DH : (h + 1) * DH].astype(F32)
            ranks = [v * meta[NT + 2 * t + r].astype(F32) for r in range(2)]
            tiles.append(jnp.concatenate(ranks, axis=1).astype(BF16))
        return jnp.concatenate(tiles, axis=0)

    def reduce_rows(h):
        key = jnp.dot(ds_s[h], masked(q_v, h), preferred_element_type=F32) * INV_ROOT
        value = jnp.dot(at_s[h], masked(g_v, h), preferred_element_type=F32)
        for hf in range(2):
            parts[h, hf, 0] = key[hf * 256 : (hf + 1) * 256].astype(BF16)
            parts[h, hf, 1] = value[hf * 256 : (hf + 1) * 256].astype(BF16)

    def merge_pair(h):
        pair_copy(h).wait_recv()
        total = (parts[h, core].astype(F32) + prx[h].astype(F32)).astype(BF16)
        for b in range(NY):
            pm[h, b] = total[:, b * 64 : (b + 1) * 64, :]
        for k in (2, 1, 3):
            y_copy(h, k, y).start()
        yrx[h, y] = pm[h, y]

    stores = []
    for h in range(NH):
        for t in range(NT):
            attend(h, t)
            if h > 0 and t == 1:
                merge_pair(h - 1)
        reduce_rows(h)
        if h == 0:
            pl.semaphore_wait(barrier, len(partners))
        pair_copy(h).start()
        store = pltpu.make_async_copy(parts.at[h], parts_hbm.at[h], store_sem.at[h])
        store.start()
        stores.append(store)
    store = pltpu.make_async_copy(qg_v, qg_hbm, store_sem.at[NH])
    store.start()
    stores.append(store)
    merge_pair(NH - 1)

    loads[6].wait()
    loads[7].wait()
    for h in range(NH):
        for k in (1, 3, 2):
            y_copy(h, k, lax.rem(y + NY - k, NY)).wait_recv()
        for gp in range(2):
            total = (yrx[h, 2 * gp].astype(F32) + yrx[h, 2 * gp + 1].astype(F32)).astype(BF16)
            for p in range(2):
                for kv in range(2):
                    x_s[
                        (gp * 2 + p) * 64 : (gp * 2 + p + 1) * 64,
                        kv * HD + h * DH : kv * HD + (h + 1) * DH,
                    ] = total[kv, :, p * DH : (p + 1) * DH]

    n = lax.broadcasted_iota(jnp.int32, (256, 256), 0)
    old = ((n >> 2) & 3) * 64 + (n >> 4) * 4 + (n & 3)
    perm = one_hot(old, lax.broadcasted_iota(jnp.int32, (256, 256), 1))
    joined = jnp.dot(perm, x_s[...], preferred_element_type=F32).astype(BF16)
    chunk = 256 // NC
    places = NZ // NC

    def project(c, target):
        piece = joined[c * chunk : (c + 1) * chunk]
        return lax.dot_general(
            piece[:, :HD], w_v[0, target], NT_DIMS, preferred_element_type=F32
        ) + lax.dot_general(piece[:, HD:], w_v[1, target], NT_DIMS, preferred_element_type=F32)

    for c in range(NC):
        for k in (2, 1, 3):
            tsend[k - 1, c] = project(c, lax.rem(x + k, NX)).astype(BF16)
            x_copy(k, c).start()
    for c in range(NC):
        town[c] = project(c, x)
    for c in range(NC):
        total = town[c]
        for k in (1, 3, 2):
            x_copy(k, c).wait_recv()
            total = total + xrx[k - 1, c].astype(F32)
        zsend[c * places : (c + 1) * places] = total.astype(BF16).reshape(places, 16, HD)
        for j in range(c * places, (c + 1) * places):
            if j < NZ - 1:
                z_copy(j, z).start()
    zrx[z] = zsend[NZ - 1]

    rows = lax.broadcasted_iota(jnp.int32, (CAPS * ROWS, 256), 0)
    cols = lax.broadcasted_iota(jnp.int32, (CAPS * ROWS, 256), 1)
    held = (capcol[...] == (rows >> 2)) & ((rows & 3) == (cols & 3))
    select = jnp.where(held, 1.0, 0.0).astype(BF16)
    for j in range(NZ - 1):
        z_copy(j, lax.rem(z + NZ - ORDER[j], NZ)).wait_recv()
    text = jnp.dot(select, zrx[...].reshape(256, HD), preferred_element_type=F32)
    text_ref[...] = text.astype(BF16)

    for h in range(NH):
        pair_copy(h).wait_send()
        for k in range(1, NY):
            y_copy(h, k, y).wait_send()
    for c in range(NC):
        for k in range(1, NX):
            x_copy(k, c).wait_send()
    for j in range(NZ - 1):
        z_copy(j, z).wait_send()
    for store in stores:
        store.wait()


def run(meta, capcol, queries, out_grad, cache, key_weight, value_weight):
    hbm = pl.BlockSpec(memory_space=pl.ANY)
    dma = pltpu.SemaphoreType.DMA
    return pl.pallas_call(
        kernel,
        out_shape=(
            jax.ShapeDtypeStruct((NT * TILE, HD), BF16),
            jax.ShapeDtypeStruct((CAPS * ROWS, HD), BF16),
            jax.ShapeDtypeStruct((NH, 2, 2, 256, 256), BF16),
        ),
        in_specs=[
            pl.BlockSpec(memory_space=pltpu.SMEM),
            pl.BlockSpec(memory_space=pltpu.VMEM),
            hbm, hbm, hbm, hbm, hbm,
        ],
        out_specs=(hbm, pl.BlockSpec(memory_space=pltpu.VMEM), hbm),
        scratch_shapes=[
            pltpu.VMEM((NT * TILE, HD), BF16),
            pltpu.VMEM((NT * TILE, HD), BF16),
            pltpu.VMEM((2, 2, L, HD), BF16),
            pltpu.VMEM((2, NH, L, 2 * DH), BF16),
            pltpu.VMEM((2, NX, HD, HD), BF16),
            pltpu.VMEM((NT * TILE, HD), BF16),
            pltpu.VMEM((NH, L, NT * TILE), BF16),
            pltpu.VMEM((NH, L, NT * TILE), BF16),
            pltpu.VMEM((NH, 2, 2, 256, 256), BF16),
            pltpu.VMEM((NH, 2, 256, 256), BF16),
            pltpu.VMEM((NH, NY, 2, 64, 256), BF16),
            pltpu.VMEM((NH, NY, 2, 64, 256), BF16),
            pltpu.VMEM((256, 2 * HD), BF16),
            pltpu.VMEM((NX - 1, NC, 256 // NC, HD), BF16),
            pltpu.VMEM((NX - 1, NC, 256 // NC, HD), BF16),
            pltpu.VMEM((NC, 256 // NC, HD), F32),
            pltpu.VMEM((NZ, 16, HD), BF16),
            pltpu.VMEM((NZ, 16, HD), BF16),
            dma((8,)),
            dma((NH + 1,)),
            dma((NH,)),
            dma((NH,)),
            dma((NH, NY - 1)),
            dma((NH, NY - 1)),
            dma((NX - 1, NC)),
            dma((NX - 1, NC)),
            dma((NZ - 1,)),
            dma((NZ - 1,)),
        ],
        compiler_params=pltpu.CompilerParams(
            collective_id=0, has_side_effects=True, vmem_limit_bytes=48 * 1024 * 1024
        ),
    )(
        meta, capcol, queries, out_grad, cache,
        key_weight.reshape(NX, HD, HD), value_weight.reshape(NX, HD, HD),
    )


def general(parts, slot_caption, key_weight, value_weight):
    z = lax.axis_index("seq") // (2 * NY)
    places = jnp.arange(NZ)
    dist = jnp.asarray(ORDER)
    order = jnp.argsort((z + dist) % NZ)
    split = parts.reshape(NH, 2, 2, NY, NZ, ROWS, 2, DH)[:, :, :, :, order]
    outgoing = split.transpose(4, 3, 1, 6, 5, 2, 0, 7).reshape(2 * NY * NZ, 2, ROWS * 2 * HD)
    received = lax.all_to_all(outgoing, "seq", split_axis=0, concat_axis=0, tiled=True)
    table = slot_caption.reshape(1, -1)
    selector = (table == jnp.arange(CAPS, dtype=jnp.int32)[:, None]).astype(BF16)
    summed = jnp.dot(selector, received.reshape(-1, ROWS * 2 * HD), preferred_element_type=F32)
    summed = summed.reshape(CAPS * ROWS, 2, HD)
    highest = lax.Precision.HIGHEST
    text = jnp.einsum("mc,dc->md", summed[:, 0], key_weight.astype(F32), precision=highest)
    text = text + jnp.einsum("mc,dc->md", summed[:, 1], value_weight.astype(F32), precision=highest)
    pieces = text.reshape(CAPS * ROWS, NX, HD).transpose(1, 0, 2)
    pieces = lax.all_to_all(pieces, "head", split_axis=0, concat_axis=0, tiled=True)
    return jnp.sum(pieces, axis=0).astype(BF16)


def shards(queries, out_grad, tile_mask, slot_caption, caption_cache, key_weight, value_weight):
    me = lax.axis_index("seq")
    groups = slot_caption.reshape(-1, GROUP * 2)
    live = groups < CAPS
    low = jnp.min(jnp.where(live, groups, CAPS), axis=1)
    high = jnp.max(jnp.where(live, groups, -1), axis=1)
    fits = jnp.all(~live | (groups == low[:, None]) | (groups == high[:, None]))
    held = jnp.stack([low, jnp.where(high > low, high, CAPS)], axis=1)
    capcol = jnp.repeat(held.reshape(1, -1), ROWS, axis=1)
    mine = lax.dynamic_slice(slot_caption, (me, 0), (1, 2))[0]
    rank = jnp.where(fits, (mine != low[me // GROUP]).astype(jnp.int32), jnp.arange(2, dtype=jnp.int32))
    mask = jnp.sum(
        tile_mask[:, :, None] * (rank[:, None] == jnp.arange(2, dtype=jnp.int32)[None, :]), axis=1
    )
    meta = jnp.concatenate([tile_mask[:, 1], mask.reshape(-1)]).astype(jnp.int32)
    query_grad, fast, parts = run(
        meta, capcol, queries, out_grad, caption_cache, key_weight, value_weight
    )
    text = lax.cond(
        fits,
        lambda f, p, s, k, v: f,
        lambda f, p, s, k, v: general(p, s, k, v),
        fast, parts, slot_caption, key_weight, value_weight,
    )
    return query_grad, text.reshape(CAPS, ROWS, HD)


def solution(mesh):
    placed = (
        P("seq", "head"),
        P("seq", "head"),
        P("seq", None),
        P(),
        P(None, "seq", None, "head"),
        P(None, "head"),
        P(None, "head"),
    )
    return jax.shard_map(
        shards,
        mesh=mesh,
        in_specs=placed,
        out_specs=(P("seq", "head"), P(None, "seq", "head")),
        check_vma=False,
    )
```

```python
import math

import jax
import jax.numpy as jnp
from jax import lax
from jax.experimental import pallas as pl
from jax.experimental.pallas import tpu as pltpu
from jax.sharding import PartitionSpec as P

DH = 128
L = 512
TILE = 128
NT = 3
NH = 3
NX = 4
NY = 4
NZ = 16
NC = 2
ROWS = 4
GROUP = 4
CAPS = 32
HD = NH * DH
INV_ROOT = 1.0 / math.sqrt(DH)
MESH = pl.DeviceIdType.MESH
F32 = jnp.float32
BF16 = jnp.bfloat16
NT_DIMS = (((1,), (1,)), ((), ()))
TN_DIMS = (((0,), (0,)), ((), ()))
ORDER = [NZ // 2 + j // 2 if j % 2 == 0 else NZ // 2 - (j + 1) // 2 for j in range(NZ)]


def one_hot(rows, columns):
    return jnp.where(rows == columns, 1.0, 0.0).astype(BF16)


def kernel(
    slots_s, tiles_s, slots_v, q_hbm, g_hbm, cache_hbm, kw_hbm, vw_hbm,
    qg_hbm, text_ref, parts_hbm, crowded,
    q_v, g_v, raw, kvp, w_v, qg_v, ds_s, at_s, parts, prx, pm, yrx, x_s, tsend, xrx, town, zsend, zrx,
    load_sem, store_sem, ps, pr, ys, yr, xs, xr, zs, zr,
):
    seq = lax.axis_index("seq")
    x = lax.axis_index("head")
    core = lax.rem(seq, 2)
    y = lax.rem(seq // 2, NY)
    z = seq // (2 * NY)

    def seq_of(z_, y_, core_):
        return (z_ * NY + y_) * 2 + core_

    pair_id = (seq_of(z, y, 1 - core), x)
    y_ids = [(seq_of(z, lax.rem(y + k, NY), core), x) for k in range(1, NY)]
    x_ids = [(seq, lax.rem(x + k, NX)) for k in range(1, NX)]
    z_ids = [(seq_of(lax.rem(z + k, NZ), y, core), x) for k in ORDER[:-1]]

    loads = []
    for kv in range(2):
        for s in range(2):
            loads.append(
                pltpu.make_async_copy(cache_hbm.at[kv, s], raw.at[kv, s], load_sem.at[kv * 2 + s])
            )
    loads.append(pltpu.make_async_copy(q_hbm, q_v, load_sem.at[4]))
    loads.append(pltpu.make_async_copy(g_hbm, g_v, load_sem.at[5]))
    loads.append(pltpu.make_async_copy(kw_hbm, w_v.at[0], load_sem.at[6]))
    loads.append(pltpu.make_async_copy(vw_hbm, w_v.at[1], load_sem.at[7]))
    for load in loads:
        load.start()

    barrier = pltpu.get_barrier_semaphore()
    partners = [pair_id] + y_ids + x_ids + z_ids
    for partner in partners:
        pl.semaphore_signal(barrier, inc=1, device_id=partner, device_id_type=MESH)

    base = (seq // GROUP) * GROUP
    near = [slots_s[s, base + j] for j in range(GROUP) for s in range(2)]
    low, high = CAPS, -1
    for c in near:
        low = jnp.minimum(low, c)
        high = jnp.maximum(high, jnp.where(c < CAPS, c, -1))
    extra = 0
    for c in near:
        extra = extra + jnp.where((c < CAPS) & (c != low) & (c != high), 1, 0)
    rank = [
        jnp.where(extra == 0, jnp.where(slots_s[s, seq] != low, 1, 0), s) for s in range(2)
    ]
    weights = [
        [
            sum(jnp.where(rank[s] == r, tiles_s[s, t], 0) for s in range(2)).astype(F32)
            for r in range(2)
        ]
        for t in range(NT)
    ]

    n = lax.broadcasted_iota(jnp.int32, (L, L), 0)
    place = (n >> 2) & (NZ - 1)
    half = place >> 1
    dist = jnp.where((place & 1) == 0, NZ // 2 + half, NZ // 2 - 1 - half)
    zdest = (z + dist) & (NZ - 1)
    old = zdest * 32 + ((n >> 6) & 3) * 8 + (n >> 8) * 4 + (n & 3)
    perm = one_hot(old, lax.broadcasted_iota(jnp.int32, (L, L), 1))
    for kv in range(2):
        for s in range(2):
            loads[kv * 2 + s].wait()
            moved = jnp.dot(perm, raw[kv, s], preferred_element_type=F32).astype(BF16)
            for h in range(NH):
                kvp[s, h, :, kv * DH : (kv + 1) * DH] = moved[:, h * DH : (h + 1) * DH]
    loads[4].wait()
    loads[5].wait()

    def pair_copy(h):
        return pltpu.make_async_remote_copy(
            src_ref=parts.at[h, 1 - core], dst_ref=prx.at[h],
            send_sem=ps.at[h], recv_sem=pr.at[h],
            device_id=pair_id, device_id_type=MESH,
        )

    def y_copy(h, k, source):
        return pltpu.make_async_remote_copy(
            src_ref=pm.at[h, lax.rem(y + k, NY)], dst_ref=yrx.at[h, source],
            send_sem=ys.at[h, k - 1], recv_sem=yr.at[h, k - 1],
            device_id=y_ids[k - 1], device_id_type=MESH,
        )

    def x_copy(k, c):
        return pltpu.make_async_remote_copy(
            src_ref=tsend.at[k - 1, c], dst_ref=xrx.at[k - 1, c],
            send_sem=xs.at[k - 1, c], recv_sem=xr.at[k - 1, c],
            device_id=x_ids[k - 1], device_id_type=MESH,
        )

    def z_copy(j, source):
        return pltpu.make_async_remote_copy(
            src_ref=zsend.at[j], dst_ref=zrx.at[source],
            send_sem=zs.at[j], recv_sem=zr.at[j],
            device_id=z_ids[j], device_id_type=MESH,
        )

    def attend(h, t):
        rows = slice(t * TILE, (t + 1) * TILE)
        cols = slice(h * DH, (h + 1) * DH)
        kv = kvp[tiles_s[1, t], h]
        q = q_v[rows, cols]
        g = g_v[rows, cols]
        zero = jnp.zeros_like(q)
        both = jnp.concatenate(
            [jnp.concatenate([q, zero], axis=1), jnp.concatenate([zero, g], axis=1)], axis=0
        )
        res = lax.dot_general(kv, both, NT_DIMS, preferred_element_type=F32)
        scores = res[:, :TILE] * INV_ROOT
        grads = res[:, TILE:]
        e = jnp.exp(scores - jnp.max(scores, axis=0, keepdims=True))
        att = e * (1.0 / jnp.sum(e, axis=0, keepdims=True))
        att_lo = att.astype(BF16)
        row_dot = jnp.sum(att_lo.astype(F32) * grads, axis=0, keepdims=True)
        ds = (att * (grads - row_dot)).astype(BF16)
        at_s[h, :, rows] = att_lo
        ds_s[h, :, rows] = ds
        qg = lax.dot_general(ds, kv[:, :DH], TN_DIMS, preferred_element_type=F32) * INV_ROOT
        qg_v[rows, cols] = qg.astype(BF16)

    def masked(ref, h):
        tiles = []
        for t in range(NT):
            v = ref[t * TILE : (t + 1) * TILE, h * DH : (h + 1) * DH].astype(F32)
            ranks = [v * weights[t][r] for r in range(2)]
            tiles.append(jnp.concatenate(ranks, axis=1).astype(BF16))
        return jnp.concatenate(tiles, axis=0)

    def reduce_rows(h):
        key = jnp.dot(ds_s[h], masked(q_v, h), preferred_element_type=F32) * INV_ROOT
        value = jnp.dot(at_s[h], masked(g_v, h), preferred_element_type=F32)
        for hf in range(2):
            parts[h, hf, 0] = key[hf * 256 : (hf + 1) * 256].astype(BF16)
            parts[h, hf, 1] = value[hf * 256 : (hf + 1) * 256].astype(BF16)

    def merge_pair(h):
        pair_copy(h).wait_recv()
        total = (parts[h, core].astype(F32) + prx[h].astype(F32)).astype(BF16)
        for b in range(NY):
            pm[h, b] = total[:, b * 64 : (b + 1) * 64, :]
        for k in (2, 1, 3):
            y_copy(h, k, y).start()
        yrx[h, y] = pm[h, y]

    stores = []
    for h in range(NH):
        for t in range(NT):
            attend(h, t)
            if h > 0 and t == 1:
                merge_pair(h - 1)
        reduce_rows(h)
        if h == 0:
            pl.semaphore_wait(barrier, len(partners))
        pair_copy(h).start()
        store = pltpu.make_async_copy(parts.at[h], parts_hbm.at[h], store_sem.at[h])
        store.start()
        stores.append(store)
    store = pltpu.make_async_copy(qg_v, qg_hbm, store_sem.at[NH])
    store.start()
    stores.append(store)
    merge_pair(NH - 1)

    loads[6].wait()
    loads[7].wait()
    for h in range(NH):
        for k in (1, 3, 2):
            y_copy(h, k, lax.rem(y + NY - k, NY)).wait_recv()
        for gp in range(2):
            total = (yrx[h, 2 * gp].astype(F32) + yrx[h, 2 * gp + 1].astype(F32)).astype(BF16)
            for p in range(2):
                for kv in range(2):
                    x_s[
                        (gp * 2 + p) * 64 : (gp * 2 + p + 1) * 64,
                        kv * HD + h * DH : kv * HD + (h + 1) * DH,
                    ] = total[kv, :, p * DH : (p + 1) * DH]

    n = lax.broadcasted_iota(jnp.int32, (256, 256), 0)
    old = ((n >> 2) & 3) * 64 + (n >> 4) * 4 + (n & 3)
    perm = one_hot(old, lax.broadcasted_iota(jnp.int32, (256, 256), 1))
    joined = jnp.dot(perm, x_s[...], preferred_element_type=F32).astype(BF16)
    chunk = 256 // NC
    places = NZ // NC

    def project(c, target):
        piece = joined[c * chunk : (c + 1) * chunk]
        return lax.dot_general(
            piece[:, :HD], w_v[0, target], NT_DIMS, preferred_element_type=F32
        ) + lax.dot_general(piece[:, HD:], w_v[1, target], NT_DIMS, preferred_element_type=F32)

    for c in range(NC):
        for k in (2, 1, 3):
            tsend[k - 1, c] = project(c, lax.rem(x + k, NX)).astype(BF16)
            x_copy(k, c).start()
    for c in range(NC):
        town[c] = project(c, x)
    for c in range(NC):
        total = town[c]
        for k in (1, 3, 2):
            x_copy(k, c).wait_recv()
            total = total + xrx[k - 1, c].astype(F32)
        zsend[c * places : (c + 1) * places] = total.astype(BF16).reshape(places, 16, HD)
        for j in range(c * places, (c + 1) * places):
            if j < NZ - 1:
                z_copy(j, z).start()
    zrx[z] = zsend[NZ - 1]

    lane = lax.broadcasted_iota(jnp.int32, (8, 128), 1)
    slot = [jnp.broadcast_to(slots_v[s : s + 1, :], (8, 128)) for s in range(2)]

    def over_group(pick, v):
        for b in (1, 2):
            other = jnp.where((lane & b) == 0, pltpu.roll(v, 128 - b, 1), pltpu.roll(v, b, 1))
            v = pick(v, other)
        return v

    low = over_group(jnp.minimum, jnp.minimum(slot[0], slot[1]))
    high = [jnp.where(v < CAPS, v, -1) for v in slot]
    high = over_group(jnp.maximum, jnp.maximum(high[0], high[1]))
    third = [jnp.where((v < CAPS) & (v != low) & (v != high), 1.0, 0.0) for v in slot]
    crowded[0] = jnp.max(jnp.maximum(third[0], third[1])).astype(jnp.int32)
    high = jnp.where(high > low, high, CAPS)
    spread = one_hot(
        lax.broadcasted_iota(jnp.int32, (128, 256), 0),
        (lax.broadcasted_iota(jnp.int32, (128, 256), 1) >> 3) * GROUP,
    )
    low = jnp.dot(low.astype(F32).astype(BF16), spread, preferred_element_type=F32)
    high = jnp.dot(high.astype(F32).astype(BF16), spread, preferred_element_type=F32)
    second = (lax.broadcasted_iota(jnp.int32, (8, 256), 1) & 4) != 0
    capcol = jnp.where(second, high, low)[0:1]

    rows = lax.broadcasted_iota(jnp.int32, (CAPS * ROWS, 256), 0)
    cols = lax.broadcasted_iota(jnp.int32, (CAPS * ROWS, 256), 1)
    held = (capcol == (rows >> 2).astype(F32)) & ((rows & 3) == (cols & 3))
    select = jnp.where(held, 1.0, 0.0).astype(BF16)
    for j in range(NZ - 1):
        z_copy(j, lax.rem(z + NZ - ORDER[j], NZ)).wait_recv()
    text = jnp.dot(select, zrx[...].reshape(256, HD), preferred_element_type=F32)
    text_ref[...] = text.astype(BF16)

    for h in range(NH):
        pair_copy(h).wait_send()
        for k in range(1, NY):
            y_copy(h, k, y).wait_send()
    for c in range(NC):
        for k in range(1, NX):
            x_copy(k, c).wait_send()
    for j in range(NZ - 1):
        z_copy(j, z).wait_send()
    for store in stores:
        store.wait()


def run(slots, tiles, queries, out_grad, cache, key_weight, value_weight):
    hbm = pl.BlockSpec(memory_space=pl.ANY)
    dma = pltpu.SemaphoreType.DMA
    return pl.pallas_call(
        kernel,
        out_shape=(
            jax.ShapeDtypeStruct((NT * TILE, HD), BF16),
            jax.ShapeDtypeStruct((CAPS * ROWS, HD), BF16),
            jax.ShapeDtypeStruct((NH, 2, 2, 256, 256), BF16),
            jax.ShapeDtypeStruct((1,), jnp.int32),
        ),
        in_specs=[
            pl.BlockSpec(memory_space=pltpu.SMEM),
            pl.BlockSpec(memory_space=pltpu.SMEM),
            pl.BlockSpec(memory_space=pltpu.VMEM),
            hbm, hbm, hbm, hbm, hbm,
        ],
        out_specs=(
            hbm,
            pl.BlockSpec(memory_space=pltpu.VMEM),
            hbm,
            pl.BlockSpec(memory_space=pltpu.SMEM),
        ),
        scratch_shapes=[
            pltpu.VMEM((NT * TILE, HD), BF16),
            pltpu.VMEM((NT * TILE, HD), BF16),
            pltpu.VMEM((2, 2, L, HD), BF16),
            pltpu.VMEM((2, NH, L, 2 * DH), BF16),
            pltpu.VMEM((2, NX, HD, HD), BF16),
            pltpu.VMEM((NT * TILE, HD), BF16),
            pltpu.VMEM((NH, L, NT * TILE), BF16),
            pltpu.VMEM((NH, L, NT * TILE), BF16),
            pltpu.VMEM((NH, 2, 2, 256, 256), BF16),
            pltpu.VMEM((NH, 2, 256, 256), BF16),
            pltpu.VMEM((NH, NY, 2, 64, 256), BF16),
            pltpu.VMEM((NH, NY, 2, 64, 256), BF16),
            pltpu.VMEM((256, 2 * HD), BF16),
            pltpu.VMEM((NX - 1, NC, 256 // NC, HD), BF16),
            pltpu.VMEM((NX - 1, NC, 256 // NC, HD), BF16),
            pltpu.VMEM((NC, 256 // NC, HD), F32),
            pltpu.VMEM((NZ, 16, HD), BF16),
            pltpu.VMEM((NZ, 16, HD), BF16),
            dma((8,)),
            dma((NH + 1,)),
            dma((NH,)),
            dma((NH,)),
            dma((NH, NY - 1)),
            dma((NH, NY - 1)),
            dma((NX - 1, NC)),
            dma((NX - 1, NC)),
            dma((NZ - 1,)),
            dma((NZ - 1,)),
        ],
        compiler_params=pltpu.CompilerParams(
            collective_id=0, has_side_effects=True, vmem_limit_bytes=67043328
        ),
    )(
        slots, tiles, slots, queries, out_grad, cache,
        key_weight.reshape(NX, HD, HD), value_weight.reshape(NX, HD, HD),
    )


def general(parts, slot_caption, key_weight, value_weight):
    z = lax.axis_index("seq") // (2 * NY)
    places = jnp.arange(NZ)
    dist = jnp.asarray(ORDER)
    order = jnp.argsort((z + dist) % NZ)
    split = parts.reshape(NH, 2, 2, NY, NZ, ROWS, 2, DH)[:, :, :, :, order]
    outgoing = split.transpose(4, 3, 1, 6, 5, 2, 0, 7).reshape(2 * NY * NZ, 2, ROWS * 2 * HD)
    received = lax.all_to_all(outgoing, "seq", split_axis=0, concat_axis=0, tiled=True)
    groups = slot_caption.reshape(-1, GROUP * 2)
    low = jnp.min(groups, axis=1, keepdims=True)
    high = jnp.max(jnp.where(groups < CAPS, groups, -1), axis=1, keepdims=True)
    fits = jnp.all((groups == CAPS) | (groups == low) | (groups == high), axis=1, keepdims=True)
    ranks = jnp.concatenate([low, jnp.where(high > low, high, CAPS)], axis=1)
    table = jnp.where(fits, jnp.tile(ranks, (1, GROUP)), groups).reshape(1, -1)
    selector = (table == jnp.arange(CAPS, dtype=jnp.int32)[:, None]).astype(BF16)
    summed = jnp.dot(selector, received.reshape(-1, ROWS * 2 * HD), preferred_element_type=F32)
    summed = summed.reshape(CAPS * ROWS, 2, HD)
    highest = lax.Precision.HIGHEST
    text = jnp.einsum("mc,dc->md", summed[:, 0], key_weight.astype(F32), precision=highest)
    text = text + jnp.einsum("mc,dc->md", summed[:, 1], value_weight.astype(F32), precision=highest)
    pieces = text.reshape(CAPS * ROWS, NX, HD).transpose(1, 0, 2)
    pieces = lax.all_to_all(pieces, "head", split_axis=0, concat_axis=0, tiled=True)
    return jnp.sum(pieces, axis=0).astype(BF16)


def shards(queries, out_grad, tile_mask, slot_caption, caption_cache, key_weight, value_weight):
    query_grad, fast, parts, crowded = run(
        slot_caption.T, tile_mask.T, queries, out_grad, caption_cache, key_weight, value_weight
    )
    text = lax.cond(
        crowded[0] == 0,
        lambda f, p, s, k, v: f,
        lambda f, p, s, k, v: general(p, s, k, v),
        fast, parts, slot_caption, key_weight, value_weight,
    )
    return query_grad, text.reshape(CAPS, ROWS, HD)


def solution(mesh):
    placed = (
        P("seq", "head"),
        P("seq", "head"),
        P("seq", None),
        P(),
        P(None, "seq", None, "head"),
        P(None, "head"),
        P(None, "head"),
    )
    return jax.shard_map(
        shards,
        mesh=mesh,
        in_specs=placed,
        out_specs=(P("seq", "head"), P(None, "seq", "head")),
        check_vma=False,
    )
```

```python
import math

import jax
import jax.numpy as jnp
from jax import lax
from jax.experimental import pallas as pl
from jax.experimental.pallas import tpu as pltpu
from jax.sharding import PartitionSpec as P

DH = 128
L = 512
TILE = 128
NT = 3
NH = 3
NX = 4
NY = 4
NZ = 16
NC = 2
ROWS = 4
GROUP = 4
CAPS = 32
HD = NH * DH
HALF = 256
BLOCK = 64
STEP = 64
INV_ROOT = 1.0 / math.sqrt(DH)
MESH = pl.DeviceIdType.MESH
F32 = jnp.float32
BF16 = jnp.bfloat16
NT_DIMS = (((1,), (1,)), ((), ()))
TN_DIMS = (((0,), (0,)), ((), ()))
EXP_SCALE = INV_ROOT * math.log2(math.e)
ORDER = [4 + j // 2 if j % 2 == 0 else 4 - (j + 1) // 2 for j in range(NZ // 2)]


def one_hot(rows, columns):
    return jnp.where(rows == columns, 1.0, 0.0).astype(BF16)


def fold(pick, v):
    return pick(v.reshape(-1, 8, v.shape[-1]), axis=0)


def kernel(
    slots_s, tiles_s, slots_v, q_hbm, g_hbm, cache_hbm, kw_hbm, vw_hbm,
    qg_hbm, text_ref, parts_hbm, crowded,
    q_v, g_v, raw, w_v, qg_v, res_s, top_s, part_s, e_s, ds_s, at_s,
    parts, prx, pm, yax, ysum, ybx, ytx, x_s, t_s, xsend, xrx, zsend, zrx,
    load_sem, store_sem, ps, pr, yas, yar, ybs, ybr, ts, tr, xs, xr, zs, zr,
):
    seq = lax.axis_index("seq")
    x = lax.axis_index("head")
    core = lax.rem(seq, 2)
    y = lax.rem(seq // 2, NY)
    z = seq // (2 * NY)
    even = lax.rem(y, 2) == 0
    odd = lax.rem(core + z, 2)

    def at(z_, y_, core_):
        return ((lax.rem(z_ + NZ, NZ) * NY + lax.rem(y_, NY)) * 2 + core_, x)

    pair_id = at(z, y, 1 - core)
    mate = jnp.where(even, y + 1, y - 1)
    across = NY - 1 - y
    x_ids = [(seq, lax.rem(x + 1, NX)), (seq, lax.rem(x + NX - 1, NX))]

    loads = []
    for kv in range(2):
        for half in range(2):
            for b in range(NY):
                loads.append(
                    pltpu.make_async_copy(
                        cache_hbm.at[kv, :, :, half, b],
                        raw.at[kv, :, half, b],
                        load_sem.at[(kv * 2 + half) * NY + b],
                    )
                )
    n_cache = len(loads)
    for source, target in (
        (q_hbm, q_v), (g_hbm, g_v), (kw_hbm, w_v.at[0]), (vw_hbm, w_v.at[1])
    ):
        loads.append(pltpu.make_async_copy(source, target, load_sem.at[len(loads)]))
    for load in loads:
        load.start()

    barrier = pltpu.get_barrier_semaphore()
    sources = [pair_id]
    sources += [at(z, mate, core), at(z, across, core)]
    sources += x_ids
    sources += [at(z + 1, 0, core)]
    sources += [at(z + NZ - k, y, lax.rem(z, 2)) for k in range(1, NZ)]
    for source in sources:
        pl.semaphore_signal(barrier, inc=1, device_id=source, device_id_type=MESH)

    @pl.when(y != 2)
    def _():
        pl.semaphore_signal(
            barrier, inc=1, device_id=at(z, 2, core), device_id_type=MESH
        )

    tails = jnp.where(y == 0, NY, jnp.where(y == 2, NY - 1, 0))
    greetings = 5 + tails + NZ - 2 + 2 * odd

    base = (seq // GROUP) * GROUP
    before = lax.rem(base + slots_s.shape[1] - 1, slots_s.shape[1])
    own = jnp.minimum(slots_s[0, base + GROUP - 1], slots_s[1, base + GROUP - 1])
    prior = jnp.minimum(slots_s[0, before], slots_s[1, before])
    extra = 0
    for j in range(GROUP):
        for s in range(2):
            c = slots_s[s, base + j]
            out = (c < CAPS) & (c != own)
            if j < 2:
                out = out & (c != prior)
            extra = extra + jnp.where(out, 1, 0)
    rank = [
        jnp.where(extra == 0, jnp.where(slots_s[s, seq] != own, 1, 0), s) for s in range(2)
    ]
    weights = [
        [
            sum(jnp.where(rank[s] == r, tiles_s[s, t], 0) for s in range(2)).astype(F32)
            for r in range(2)
        ]
        for t in range(NT)
    ]

    def pair_copy(h, r):
        return pltpu.make_async_remote_copy(
            src_ref=parts.at[h, r, 1 - core], dst_ref=prx.at[h, r],
            send_sem=ps.at[h, r], recv_sem=pr.at[h, r],
            device_id=pair_id, device_id_type=MESH,
        )

    def mate_copy(h, i):
        block = NY - 1 - mate if i else mate
        return pltpu.make_async_remote_copy(
            src_ref=pm.at[h, 0, block], dst_ref=yax.at[h, i],
            send_sem=yas.at[h, i], recv_sem=yar.at[h, i],
            device_id=at(z, mate, core), device_id_type=MESH,
        )

    def across_copy(h):
        return pltpu.make_async_remote_copy(
            src_ref=ysum.at[h], dst_ref=ybx.at[h],
            send_sem=ybs.at[h], recv_sem=ybr.at[h],
            device_id=at(z, across, core), device_id_type=MESH,
        )

    def tail_copy(h, k, place):
        return pltpu.make_async_remote_copy(
            src_ref=pm.at[h, 1, lax.rem(y + k, NY)], dst_ref=ytx.at[h, place],
            send_sem=ts.at[h, k], recv_sem=tr.at[h, place],
            device_id=at(jnp.where(y == 0, z + NZ - 1, z), y + k, core), device_id_type=MESH,
        )

    def x_copy(d, m, c):
        return pltpu.make_async_remote_copy(
            src_ref=xsend.at[d, m, c], dst_ref=xrx.at[d, m, c],
            send_sem=xs.at[d, m, c], recv_sem=xr.at[d, m, c],
            device_id=x_ids[d], device_id_type=MESH,
        )

    def z_copy(j, other, source):
        c = 1 - core if other else core
        return pltpu.make_async_remote_copy(
            src_ref=zsend.at[2 * j + c], dst_ref=zrx.at[source],
            send_sem=zs.at[2 * j + other], recv_sem=zr.at[source],
            device_id=at(z + odd + 2 * ORDER[j], y, c), device_id_type=MESH,
        )

    def slot_block(h, t, kv):
        return raw[kv, tiles_s[1, t], :, :, :, :, h * DH : (h + 1) * DH].reshape(L, DH)

    def score(h, t):
        rows = slice(t * TILE, (t + 1) * TILE)
        cols = slice(h * DH, (h + 1) * DH)
        q = q_v[rows, cols]
        g = g_v[rows, cols]
        zero = jnp.zeros_like(q)
        both = jnp.concatenate(
            [jnp.concatenate([q, zero], axis=1), jnp.concatenate([zero, g], axis=1)], axis=0
        )
        res = lax.dot_general(
            jnp.concatenate([slot_block(h, t, 0), slot_block(h, t, 1)], axis=1),
            both, NT_DIMS, preferred_element_type=F32,
        )
        res_s[t] = res
        top_s[t] = fold(jnp.max, res[:, :TILE])

    def attend(h, t):
        rows = slice(t * TILE, (t + 1) * TILE)
        top = jnp.max(top_s[t], axis=0, keepdims=True)
        total = jnp.zeros((8, TILE), F32)
        dot = jnp.zeros((8, TILE), F32)
        for i in range(0, L, STEP):
            e = jnp.exp2((res_s[t, i : i + STEP, :TILE] - top) * EXP_SCALE)
            e_s[t, i : i + STEP] = e
            total = total + fold(jnp.sum, e)
            dot = dot + fold(jnp.sum, e * res_s[t, i : i + STEP, TILE:])
        inverse = 1.0 / jnp.sum(total, axis=0, keepdims=True)
        row_dot = jnp.sum(dot, axis=0, keepdims=True) * inverse
        for i in range(0, L, STEP):
            att = e_s[t, i : i + STEP] * inverse
            at_s[h, i : i + STEP, rows] = att.astype(BF16)
            ds_s[h, i : i + STEP, rows] = (
                att * (res_s[t, i : i + STEP, TILE:] - row_dot)
            ).astype(BF16)

    def query(h, t):
        rows = slice(t * TILE, (t + 1) * TILE)
        qg = lax.dot_general(
            ds_s[h, :, rows], slot_block(h, t, 0), TN_DIMS, preferred_element_type=F32
        )
        qg_v[rows, h * DH : (h + 1) * DH] = (qg * INV_ROOT).astype(BF16)

    def masked(ref, h, t):
        v = ref[t * TILE : (t + 1) * TILE, h * DH : (h + 1) * DH].astype(F32)
        return jnp.concatenate([v * weights[t][r] for r in range(2)], axis=1).astype(BF16)

    def reduce_first(h, kv):
        lhs, rhs = ((ds_s, q_v), (at_s, g_v))[kv]
        tiles = jnp.concatenate([masked(rhs, h, 0), masked(rhs, h, 1)], axis=0)
        part_s[kv] = jnp.dot(lhs[h, :, : 2 * TILE], tiles, preferred_element_type=F32)

    def reduce_last(h, kv):
        lhs, rhs = ((ds_s, q_v), (at_s, g_v))[kv]
        part = part_s[kv] + jnp.dot(
            lhs[h, :, 2 * TILE :], masked(rhs, h, 2), preferred_element_type=F32
        )
        if kv == 0:
            part = part * INV_ROOT
        for r in range(2):
            for half in range(2):
                parts[h, r, half, kv] = part[
                    half * HALF : (half + 1) * HALF, r * DH : (r + 1) * DH
                ].astype(BF16)

    def add_pair(h, r):
        pair_copy(h, r).wait_recv()
        total = (parts[h, r, core].astype(F32) + prx[h, r].astype(F32)).astype(BF16)
        for b in range(NY):
            pm[h, r, b] = total[:, b * BLOCK : (b + 1) * BLOCK, :]

    def merge_pair(h):
        add_pair(h, 0)
        for i in (1, 0):
            mate_copy(h, i).start()

        @pl.when(even)
        def _():
            add_pair(h, 1)
            for k in (2, 1, 3):
                tail_copy(h, k, y // 2).start()

            @pl.when(y == 0)
            def _():
                tail_copy(h, 0, y // 2).start()

            @pl.when(y != 0)
            def _():
                ytx[h, 1] = pm[h, 1, y]

    def join_group(h):
        mate_copy(h, 1).wait_recv()
        ysum[h] = (pm[h, 0, across].astype(F32) + yax[h, 1].astype(F32)).astype(BF16)
        across_copy(h).start()

    for load in loads[: n_cache + 2]:
        load.wait()
    stores = []
    score(0, 0)
    for h in range(NH):
        score(h, 1)
        attend(h, 0)
        score(h, 2)
        attend(h, 1)
        if h > 1:
            join_group(h - 2)
        if h > 0:
            merge_pair(h - 1)
        if h + 1 < NH:
            score(h + 1, 0)
        reduce_first(h, 1)
        reduce_first(h, 0)
        attend(h, 2)
        reduce_last(h, 1)
        reduce_last(h, 0)
        if h == 0:
            pl.semaphore_wait(barrier, greetings)
        pair_copy(h, 0).start()

        @pl.when(even)
        def _(h=h):
            pair_copy(h, 1).start()

        store = pltpu.make_async_copy(parts.at[h], parts_hbm.at[h], store_sem.at[h])
        store.start()
        stores.append(store)
    for h in range(NH - 1):
        for t in range(NT):
            query(h, t)
        if h == 0:
            join_group(NH - 2)
    merge_pair(NH - 1)
    for t in range(NT):
        query(NH - 1, t)
    store = pltpu.make_async_copy(qg_v, qg_hbm, store_sem.at[NH])
    store.start()
    stores.append(store)

    lane = lax.broadcasted_iota(jnp.int32, (8, 128), 1)
    spot = lane & (GROUP - 1)
    slot = [jnp.broadcast_to(slots_v[s : s + 1, :], (8, 128)) for s in range(2)]
    lowest = jnp.minimum(slot[0], slot[1])
    owner, earlier = lowest, lowest
    for j in range(GROUP - 1):
        owner = jnp.where(spot == j, pltpu.roll(lowest, 128 - (GROUP - 1 - j), 1), owner)
    for j in range(2):
        earlier = jnp.where(spot == j, pltpu.roll(lowest, j + 1, 1), earlier)
    third = [
        jnp.where((v < CAPS) & (v != owner) & ((v != earlier) | (spot >= 2)), 1.0, 0.0)
        for v in slot
    ]
    crowded[0] = jnp.max(jnp.maximum(third[0], third[1])).astype(jnp.int32)
    rows = lax.broadcasted_iota(jnp.int32, (CAPS * ROWS, 128), 0)
    cols = lax.broadcasted_iota(jnp.int32, (CAPS * ROWS, 128), 1)
    held = (owner[0:1] == (rows >> 2)) & ((rows & 3) == (cols & 3))
    select = jnp.where(held, 1.0, 0.0).astype(BF16)

    place = rows >> 4
    step = jnp.where((place & 1) == 0, 4 + (place >> 1), 3 - (place >> 1))
    dest = (z + odd + 2 * step) & (NZ - 1)
    old = ((rows >> 2) & 1) * BLOCK + (dest >> 1) * 8 + ((rows >> 3) & 1) * 4 + (rows & 3)
    perm = one_hot(old, cols)

    loads[n_cache + 2].wait()
    loads[n_cache + 3].wait()
    join_group(NH - 1)
    mine = y // 2
    for h in range(NH):
        tail_copy(h, 0, 0).wait_recv()

        @pl.when(y != 2)
        def _(h=h):
            tail_copy(h, 0, 1).wait_recv()

        mate_copy(h, 0).wait_recv()
        near = pm[h, 0, y].astype(F32) + yax[h, 0].astype(F32) + ytx[h, 1 - mine].astype(F32)
        across_copy(h).wait_recv()
        far = ybx[h].astype(F32) + ytx[h, mine].astype(F32)
        for kv in range(2):
            cols = slice(kv * HD + h * DH, kv * HD + (h + 1) * DH)
            x_s[mine, :, cols] = near[kv].astype(BF16)
            x_s[1 - mine, :, cols] = far[kv].astype(BF16)
    joined = jnp.dot(
        perm, x_s[...].reshape(2 * BLOCK, 2 * HD), preferred_element_type=F32
    ).astype(BF16)
    chunk = 2 * BLOCK // NC
    places = NZ // 2 // NC

    def project(target):
        return lax.dot_general(
            joined[:, :HD], w_v[0, target], NT_DIMS, preferred_element_type=F32
        ) + lax.dot_general(joined[:, HD:], w_v[1, target], NT_DIMS, preferred_element_type=F32)

    def half(c, d):
        start = c * chunk + d * (chunk // 2)
        return slice(start, start + chunk // 2)

    piece = project(lax.rem(x + 2, NX))
    for c in range(NC):
        for d in range(2):
            xsend[d, 0, c] = piece[half(c, d)].astype(BF16)
            x_copy(d, 0, c).start()
    for d in range(2):
        piece = project(lax.rem(x + (1, NX - 1)[d], NX))
        t_s[d] = piece
        for c in range(NC):
            xsend[d, 1, c] = piece[half(c, 1 - d)].astype(BF16)
            x_copy(d, 1, c).start()
    t_s[2] = project(x)
    for c in range(NC):
        for d in range(2):
            x_copy(d, 0, c).wait_recv()
            xsend[d, 2, c] = (t_s[d, half(c, d)] + xrx[d, 0, c].astype(F32)).astype(BF16)
            x_copy(d, 2, c).start()
    for c in range(NC):
        total = []
        for d in range(2):
            x_copy(1 - d, 1, c).wait_recv()
            x_copy(d, 2, c).wait_recv()
            total.append(
                t_s[2, half(c, d)] + xrx[1 - d, 1, c].astype(F32) + xrx[d, 2, c].astype(F32)
            )
        total = jnp.concatenate(total, axis=0)
        zsend[2 * c * places : 2 * (c + 1) * places] = total.reshape(2 * places, 8, HD).astype(BF16)
        for j in range(c * places, (c + 1) * places):
            z_copy(j, 1, z).start()
            if ORDER[j] > 0:
                z_copy(j, 0, z).start()
            else:

                @pl.when(odd == 1)
                def _(j=j):
                    z_copy(j, 0, z).start()

                @pl.when(odd == 0)
                def _(j=j):
                    zrx[z] = zsend[2 * j + core]

    for k in range(1, NZ):
        z_copy(0, 0, lax.rem(z + NZ - k, NZ)).wait_recv()

    @pl.when(odd == 1)
    def _():
        z_copy(0, 0, z).wait_recv()

    text = jnp.dot(select, zrx[...].reshape(128, HD), preferred_element_type=F32)
    text_ref[...] = text.astype(BF16)

    for h in range(NH):
        pair_copy(h, 0).wait_send()
        for i in range(2):
            mate_copy(h, i).wait_send()
        across_copy(h).wait_send()

        @pl.when(even)
        def _(h=h):
            pair_copy(h, 1).wait_send()
            for k in range(1, NY):
                tail_copy(h, k, y // 2).wait_send()

            @pl.when(y == 0)
            def _():
                tail_copy(h, 0, y // 2).wait_send()

    for c in range(NC):
        for d in range(2):
            for m in range(3):
                x_copy(d, m, c).wait_send()
    for j in range(NZ // 2):
        z_copy(j, 1, z).wait_send()
        if ORDER[j] > 0:
            z_copy(j, 0, z).wait_send()

    @pl.when(odd == 1)
    def _():
        z_copy(ORDER.index(0), 0, z).wait_send()

    for store in stores:
        store.wait()


def run(slots, tiles, queries, out_grad, cache, key_weight, value_weight):
    hbm = pl.BlockSpec(memory_space=pltpu.HBM)
    smem = pl.BlockSpec(memory_space=pltpu.SMEM)
    vmem = pl.BlockSpec(memory_space=pltpu.VMEM)
    dma = pltpu.SemaphoreType.DMA
    return pl.pallas_call(
        kernel,
        out_shape=(
            jax.ShapeDtypeStruct((NT * TILE, HD), BF16),
            jax.ShapeDtypeStruct((CAPS * ROWS, HD), BF16),
            jax.ShapeDtypeStruct((NH, 2, 2, 2, HALF, DH), BF16),
            jax.ShapeDtypeStruct((1,), jnp.int32),
        ),
        in_specs=[smem, smem, vmem, hbm, hbm, hbm, hbm, hbm],
        out_specs=(pl.BlockSpec(memory_space=pl.ANY), vmem, hbm, smem),
        scratch_shapes=[
            pltpu.VMEM((NT * TILE, HD), BF16),
            pltpu.VMEM((NT * TILE, HD), BF16),
            pltpu.VMEM((2, 2, 2, NY, NZ // 2, 8, HD), BF16),
            pltpu.VMEM((2, NX, HD, HD), BF16),
            pltpu.VMEM((NT * TILE, HD), BF16),
            pltpu.VMEM((NT, L, 2 * TILE), F32),
            pltpu.VMEM((NT, 8, TILE), F32),
            pltpu.VMEM((2, L, 2 * DH), F32),
            pltpu.VMEM((NT, L, TILE), F32),
            pltpu.VMEM((NH, L, NT * TILE), BF16),
            pltpu.VMEM((NH, L, NT * TILE), BF16),
            pltpu.VMEM((NH, 2, 2, 2, HALF, DH), BF16),
            pltpu.VMEM((NH, 2, 2, HALF, DH), BF16),
            pltpu.VMEM((NH, 2, NY, 2, BLOCK, DH), BF16),
            pltpu.VMEM((NH, 2, 2, BLOCK, DH), BF16),
            pltpu.VMEM((NH, 2, BLOCK, DH), BF16),
            pltpu.VMEM((NH, 2, BLOCK, DH), BF16),
            pltpu.VMEM((NH, 2, 2, BLOCK, DH), BF16),
            pltpu.VMEM((2, BLOCK, 2 * HD), BF16),
            pltpu.VMEM((3, 2 * BLOCK, HD), F32),
            pltpu.VMEM((2, 3, NC, BLOCK // NC, HD), BF16),
            pltpu.VMEM((2, 3, NC, BLOCK // NC, HD), BF16),
            pltpu.VMEM((NZ, 8, HD), BF16),
            pltpu.VMEM((NZ, 8, HD), BF16),
            dma((20,)),
            dma((NH + 1,)),
            dma((NH, 2)),
            dma((NH, 2)),
            dma((NH, 2)),
            dma((NH, 2)),
            dma((NH,)),
            dma((NH,)),
            dma((NH, NY)),
            dma((NH, 2)),
            dma((2, 3, NC)),
            dma((2, 3, NC)),
            dma((NZ,)),
            dma((NZ,)),
        ],
        compiler_params=pltpu.CompilerParams(
            collective_id=0, has_side_effects=True, vmem_limit_bytes=67043328
        ),
    )(
        slots, tiles, slots, queries, out_grad,
        cache.reshape(2, 2, NZ // 2, 2, NY, 8, HD),
        key_weight.reshape(NX, HD, HD), value_weight.reshape(NX, HD, HD),
    )


def general(parts, slot_caption, key_weight, value_weight):
    split = parts.reshape(NH, 2, 2, 2, NY, NZ // 2, 2, ROWS, DH)
    outgoing = split.transpose(5, 2, 4, 6, 1, 7, 3, 0, 8).reshape(-1, 2, ROWS * 2 * HD)
    received = lax.all_to_all(outgoing, "seq", split_axis=0, concat_axis=0, tiled=True)
    groups = slot_caption.reshape(-1, GROUP * 2)
    owner = jnp.min(groups[:, -2:], axis=1, keepdims=True)
    earlier = jnp.roll(owner, 1, axis=0)
    early = jnp.arange(GROUP * 2)[None, :] < 4
    fits = jnp.all(
        (groups == CAPS) | (groups == owner) | ((groups == earlier) & early), axis=1, keepdims=True
    )
    ranks = jnp.concatenate([owner, earlier], axis=1)
    table = jnp.where(fits, jnp.tile(ranks, (1, GROUP)), groups).reshape(1, -1)
    selector = (table == jnp.arange(CAPS, dtype=jnp.int32)[:, None]).astype(BF16)
    summed = jnp.dot(selector, received.reshape(-1, ROWS * 2 * HD), preferred_element_type=F32)
    summed = summed.reshape(CAPS * ROWS, 2, HD)
    highest = lax.Precision.HIGHEST
    text = jnp.einsum("mc,dc->md", summed[:, 0], key_weight.astype(F32), precision=highest)
    text = text + jnp.einsum("mc,dc->md", summed[:, 1], value_weight.astype(F32), precision=highest)
    pieces = text.reshape(CAPS * ROWS, NX, HD).transpose(1, 0, 2)
    pieces = lax.all_to_all(pieces, "head", split_axis=0, concat_axis=0, tiled=True)
    return jnp.sum(pieces, axis=0).astype(BF16)


def shards(queries, out_grad, tile_mask, slot_caption, caption_cache, key_weight, value_weight):
    query_grad, fast, parts, crowded = run(
        slot_caption.T, tile_mask.T, queries, out_grad, caption_cache, key_weight, value_weight
    )
    text = lax.cond(
        crowded[0] == 0,
        lambda f, p, s, k, v: f,
        lambda f, p, s, k, v: general(p, s, k, v),
        fast, parts, slot_caption, key_weight, value_weight,
    )
    return query_grad, text.reshape(CAPS, ROWS, HD)


def solution(mesh):
    placed = (
        P("seq", "head"),
        P("seq", "head"),
        P("seq", None),
        P(),
        P(None, "seq", None, "head"),
        P(None, "head"),
        P(None, "head"),
    )
    return jax.shard_map(
        shards,
        mesh=mesh,
        in_specs=placed,
        out_specs=(P("seq", "head"), P(None, "seq", "head")),
        check_vma=False,
    )
```
